1024 devices in a mesh: cuts: 4 (over x_lo, core), dp: 16 (over y, x_hi), tensor: 16 (over z).
Axes of the slice: x: 4 (x_hi: 2, x_lo: 2; x = x_hi * 2 + x_lo), y: 8, z: 16, core: 2. Of those that a mesh axis runs over, the one named last changes fastest.
Arguments:
- grad_out: bfloat16 [65536, 4096], P(('cuts', 'dp')), may hold values from -16 to 16
- attn_out: bfloat16 [65536, 4096], P(('cuts', 'dp'), 'tensor'), may hold values from -6 to 6
Outputs:
- grad_weight: float32 [4096, 4096], P(('cuts', 'dp'), 'tensor')
The draws below stay inside these ranges and needn't reach their ends.
All inputs are finite; a program needn't handle non-finite values.
Results may differ from the reference program's by a relative error of at most 0.0003.
Values sent between devices are 32-bit elements; how exact they have to be, the bound alone decides.
No kernel may reach another device: no remote copies, remote signals or barrier semaphores. Data moves between devices by JAX's collectives and lax.ppermute only.
A program may use at most 32 MiB of HBM per device.

```python
import jax
import jax.numpy as jnp
from jax import lax

D = 4096
ATT = 4096
TOKENS = 65536


def spiked(values, stream_key, source, target, blocks, factor):
    def block_of(axis_at):
        return (jnp.arange(values.shape[axis_at]) // (values.shape[axis_at] // blocks)).reshape((-1,) + (1,) * (values.ndim - 1 - axis_at))

    near = jax.random.permutation(stream_key, blocks)[block_of(target)]
    second = (block_of(target) + blocks // 2) % blocks
    return jnp.where((block_of(source) == near) | (block_of(source) == second), factor * values, values)


def levels(own_key, dims, split, least, top_value):
    gain, own = 1.0, jax.random.fold_in(own_key, 6)
    for dim, blocks in split:
        heights = jnp.exp(jax.random.uniform(jax.random.fold_in(own, dim), (blocks,), jnp.float32, least / len(split), top_value / len(split)))
        gain = gain * jnp.repeat(heights, dims[dim] // blocks).reshape([-1 if axis == dim else 1 for axis in range(len(dims))])
    return gain


def centred(own_key, shape, spread, most, shards=(), held_as=jnp.bfloat16):
    drawn = jax.random.normal(own_key, shape, jnp.float32) * spread
    if len(shards) > 0:
        drawn = levels(own_key, shape, shards, -0.22, 0.18) * drawn
    return jnp.clip(drawn, min=-most, max=most).astype(held_as)


def heavy_noise(rng, shape, scale, reach, cuts, heavy, kind=jnp.bfloat16):
    drawn = scale * jax.random.normal(rng, shape, jnp.float32)
    if cuts:
        drawn = drawn * levels(rng, shape, cuts, -0.22, 0.18)
    return jnp.clip(spiked(drawn, jax.random.fold_in(rng, 3), *heavy), -reach, reach).astype(kind)


def setup_inputs(seed: int = 0) -> dict:
    key_of = jax.random.split(jax.random.key(seed), 3)
    grad_out = heavy_noise(key_of[0], (TOKENS, D), 1.0, 16.0, ((0, 64),), (0, 1, 64, 4.0))
    attn_out = centred(key_of[1], (TOKENS, ATT), 1.0, 6.0, ((0, 64), (1, 16)))
    return {"grad_out": grad_out, "attn_out": attn_out}


def reference(grad_out, attn_out):
    summed = lax.dot_general(grad_out, attn_out, (((0,), (0,)), ((), ())), preferred_element_type=jnp.float32)
    return summed / jnp.sqrt(jnp.float32(TOKENS))
```

```python
import math

import jax
import jax.numpy as jnp
from jax import lax
from jax.sharding import Mesh, PartitionSpec as P

CHIP_ORDER = ("y", "xh", "xl", "core")
OWNERS = ("xl", "core", "y", "xh")


def body(grad_out, attn_out):
    sizes = {axis: lax.axis_size(axis) for axis in OWNERS}
    shards = math.prod(sizes.values())
    factor = 1.0 / math.sqrt(float(grad_out.shape[0] * shards))
    partial = lax.dot_general(
        grad_out, attn_out, (((0,), (0,)), ((), ())), preferred_element_type=jnp.float32
    )
    rows, columns = partial.shape[0] // shards, partial.shape[1]
    blocks = partial.reshape(tuple(sizes[axis] for axis in OWNERS) + (rows, columns))
    order = tuple(OWNERS.index(axis) for axis in CHIP_ORDER)
    blocks = blocks.transpose(order + (4, 5)).reshape(shards * rows, columns)
    summed = lax.psum_scatter(blocks, CHIP_ORDER, scatter_dimension=0, tiled=True)
    return summed * factor


def solution(mesh):
    cuts, dp, tensor = mesh.devices.shape
    parts = mesh.devices.reshape(2, cuts // 2, dp // 2, 2, tensor)
    chips = Mesh(parts, OWNERS + ("z",))
    placed = (P(OWNERS, None), P(OWNERS, "z"))
    return jax.shard_map(body, mesh=chips, in_specs=placed, out_specs=P(OWNERS, "z"), check_vma=False)
```

```python
import functools
import math

import jax
import jax.numpy as jnp
from jax import lax
from jax.experimental import pallas as pl
from jax.experimental.pallas import tpu as pltpu
from jax.sharding import Mesh, PartitionSpec as P


X, Y = 4, 8
WIDE = 512


def place(g):
    return (g & 1) * 2 + (g >> 5), (g >> 1) & 7, (g >> 4) & 1


def position(x, y, core):
    return (((x % 2) * 2 + core) * Y + y) * 2 + x // 2


def rank(x, y):
    return (x % 2) * 16 + (y % 2) * 8 + (x // 2) * 4 + ((y // 2) % 2) * 2 + y // 4


def send(value, dx, dy):
    pairs = []
    for g in range(2 * X * Y):
        x, y, core = place(g)
        far = (((x - core) % X ^ dx) + core) % X, (((y - core) % Y ^ dy) + core) % Y
        pairs.append((g, position(*far, core)))
    return lax.ppermute(value, "g", pairs)


def mine(other):
    x, y, core = place(lax.axis_index("g"))
    core = core ^ other
    return core, (x - core) & 3, (y - core) & 7


def half_kernel(other, grad_ref, attn_ref, out_ref):
    core, my_x, my_y = mine(other)
    x_low, step = pl.program_id(0), pl.program_id(1)
    for k in range(WIDE // 128):
        block = lax.dot_general(
            grad_ref[:, k * 128 : (k + 1) * 128],
            attn_ref[...],
            (((0,), (0,)), ((), ())),
            preferred_element_type=jnp.float32,
        )
        y = ((step * (WIDE // 128) + k - core) & 7) ^ my_y
        for x_high in range(2):
            x = ((x_high * 2 + x_low - core) & 3) ^ my_x
            at = (y & 1) * 8 + (x >> 1) * 4 + ((y >> 1) & 1) * 2 + (y >> 2)
            out_ref[at] = block[x_high * 64 : (x_high + 1) * 64, :]


def half(grad_out, attn_out, other):
    tokens, columns = attn_out.shape
    steps = grad_out.shape[1] // 4 // WIDE

    def grad_map(i, j):
        core, _, _ = mine(other)
        return 0, (i * 2 + core) * steps + j

    def out_map(i, j):
        core, my_x, _ = mine(other)
        return ((i - core) ^ my_x) & 1, 0, 0

    return pl.pallas_call(
        functools.partial(half_kernel, other),
        out_shape=jax.ShapeDtypeStruct((X * Y, 64, columns), jnp.float32),
        grid=(2, steps),
        in_specs=[
            pl.BlockSpec((tokens, WIDE), grad_map),
            pl.BlockSpec((tokens, columns), lambda i, j: (0, 0)),
        ],
        out_specs=pl.BlockSpec((X * Y // 2, 64, columns), out_map),
        compiler_params=pltpu.CompilerParams(
            dimension_semantics=("arbitrary", "arbitrary"), vmem_limit_bytes=16 << 20
        ),
        cost_estimate=pl.CostEstimate(
            flops=tokens * grad_out.shape[1] * columns,
            bytes_accessed=tokens * grad_out.shape[1] + (X * Y * 64 * columns) * 4,
            transcendentals=0,
        ),
    )(grad_out, attn_out)


def body(grad_out, attn_out):
    factor = 1.0 / math.sqrt(float(grad_out.shape[0] * lax.axis_size("g")))
    grad_out = pltpu.with_memory_space_constraint(grad_out, pltpu.HBM)
    theirs = half(grad_out, attn_out, 1)
    got = lax.ppermute(theirs, "g", [(s, s ^ 16) for s in range(2 * X * Y)])
    total = half(grad_out, attn_out, 0) + got
    for far_x, far_y in ((1, 1), (2, 2), (0, 4)):
        kept = total.shape[0] // (4 if far_x else 2)
        others = [(far_x, far_y), (far_x, 0), (0, far_y)] if far_x else [(0, far_y)]
        came = []
        for dx, dy in others:
            at = rank(dx, dy)
            came.append(send(total[at : at + kept], dx, dy))
        total = total[:kept]
        for term in came:
            total = total + term
    return total[0] * factor


def solution(mesh):
    cuts, dp, tensor = mesh.devices.shape
    flat = Mesh(mesh.devices.reshape(cuts * dp, tensor), ("g", "z"))
    placed = (P("g", None), P("g", "z"))
    return jax.shard_map(body, mesh=flat, in_specs=placed, out_specs=P("g", "z"), check_vma=False)
```

```python
import functools
import math

import jax
import jax.numpy as jnp
from jax import lax
from jax.experimental import pallas as pl
from jax.experimental.pallas import tpu as pltpu
from jax.sharding import Mesh, PartitionSpec as P


X, Y = 4, 8
COPIES = 4


def place(g):
    return (g & 1) * 2 + (g >> 5), (g >> 1) & 7, (g >> 4) & 1


def position(x, y, core):
    return (((x % 2) * 2 + core) * Y + y) * 2 + x // 2


def position_of(label_x, label_y, core):
    return position((label_x + core) % X, (label_y + core) % Y, core)


def near(value, dx, dy):
    pairs = []
    for g in range(2 * X * Y):
        x, y, core = place(g)
        pairs.append((g, position_of((x - core) % X ^ dx, (y - core) % Y ^ dy, core)))
    return lax.ppermute(value, "g", pairs)


def far(value):
    groups = [
        [position_of(x_low + 2 * (at >> 2), y_low + 2 * (at & 3), core) for at in range(8)]
        for core in range(2)
        for x_low in range(2)
        for y_low in range(2)
    ]
    return lax.all_to_all(value, "g", 0, 0, axis_index_groups=groups, tiled=True)


def half_kernel(other, grad_hbm, attn_hbm, out_ref, grad, attn, grad_sems, attn_sem):
    x, y, core = place(lax.axis_index("g"))
    core = core ^ other
    my_x, my_y = (x - core) & 3, (y - core) & 7
    tokens, run = grad.shape[1:]
    copies = [pltpu.make_async_copy(attn_hbm, attn, attn_sem)]
    copies[0].start()
    for x_low in range(2):
        columns = pl.ds(pl.multiple_of((x_low * 2 + core) * run, run), run)
        for part in range(COPIES):
            rows = pl.ds(part * (tokens // COPIES), tokens // COPIES)
            copy = pltpu.make_async_copy(
                grad_hbm.at[rows, columns], grad.at[x_low, rows, :], grad_sems.at[x_low, part]
            )
            copy.start()
            copies.append(copy)
    copies[0].wait()
    for x_low in range(2):
        for part in range(COPIES):
            copies[1 + x_low * COPIES + part].wait()
        for k in range(Y):
            block = lax.dot_general(
                grad[x_low, :, k * 128 : (k + 1) * 128],
                attn[...],
                (((0,), (0,)), ((), ())),
                preferred_element_type=jnp.float32,
            )
            label_y = (k - core) & 7
            for x_high in range(2):
                label_x = (x_high * 2 + x_low - core) & 3
                at = ((label_x ^ my_x) & 1) * 16 + ((label_y ^ my_y) & 1) * 8 + (label_x >> 1) * 4 + (label_y >> 1)
                out_ref[at] = block[x_high * 64 : (x_high + 1) * 64, :]


def half(grad_out, attn_out, other):
    tokens, columns = attn_out.shape
    run = grad_out.shape[1] // 4
    return pl.pallas_call(
        functools.partial(half_kernel, other),
        out_shape=jax.ShapeDtypeStruct((X * Y, run // 16, columns), jnp.float32),
        in_specs=[pl.BlockSpec(memory_space=pltpu.HBM)] * 2,
        out_specs=pl.BlockSpec(memory_space=pltpu.VMEM),
        scratch_shapes=[
            pltpu.VMEM((2, tokens, run), jnp.bfloat16),
            pltpu.VMEM((tokens, columns), jnp.bfloat16),
            pltpu.SemaphoreType.DMA((2, COPIES)),
            pltpu.SemaphoreType.DMA,
        ],
        compiler_params=pltpu.CompilerParams(vmem_limit_bytes=16 << 20),
        cost_estimate=pl.CostEstimate(
            flops=4 * tokens * run * columns,
            bytes_accessed=4 * tokens * run + 2 * tokens * columns + 8 * run * columns,
            transcendentals=0,
        ),
    )(grad_out, attn_out)


def body(grad_out, attn_out):
    factor = 1.0 / math.sqrt(float(grad_out.shape[0] * lax.axis_size("g")))
    grad_out, attn_out = (pltpu.with_memory_space_constraint(v, pltpu.HBM) for v in (grad_out, attn_out))
    theirs = half(grad_out, attn_out, 1)
    got = lax.ppermute(theirs, "g", [(s, s ^ 16) for s in range(2 * X * Y)])
    total = half(grad_out, attn_out, 0) + got
    came = [near(total[24:32], 1, 1), near(total[16:24], 1, 0), near(total[8:16], 0, 1)]
    total = total[:8] + came[0] + came[1] + came[2]
    terms = far(total)
    total = terms[0]
    for at in range(1, terms.shape[0]):
        total = total + terms[at]
    return total * factor


def solution(mesh):
    cuts, dp, tensor = mesh.devices.shape
    flat = Mesh(mesh.devices.reshape(cuts * dp, tensor), ("g", "z"))
    placed = (P("g", None), P("g", "z"))
    return jax.shard_map(body, mesh=flat, in_specs=placed, out_specs=P("g", "z"), check_vma=False)
```

```python
import functools
import math

import jax
import jax.numpy as jnp
from jax import lax
from jax.experimental import pallas as pl
from jax.experimental.pallas import tpu as pltpu
from jax.sharding import Mesh, PartitionSpec as P


X, Y = 4, 8
COPIES = 2


def place(g):
    return (g & 1) * 2 + (g >> 5), (g >> 1) & 7, (g >> 4) & 1


def position(x, y, core):
    return (((x % 2) * 2 + core) * Y + y) * 2 + x // 2


def colour(x, y, core):
    return (x * (1 - 2 * core) + y * 2) & 3


def near(value, apart):
    dx, dy = {1: (1, 0), 2: (0, 1), 3: (-1, 0)}[apart]
    pairs = []
    for g in range(2 * X * Y):
        x, y, core = place(g)
        to = (x + dx * (1 - 2 * core)) % X, (y + dy * (1 - 2 * core)) % Y
        assert (colour(*to, core) - colour(x, y, core)) % 4 == apart
        pairs.append((g, position(*to, core)))
    return lax.ppermute(value, "g", pairs)


def far(value):
    groups = [[0] * 8 for _ in range(8)]
    for g in range(2 * X * Y):
        x, y, core = place(g)
        groups[core * 4 + colour(x, y, core)][y] = g
    return lax.all_to_all(value, "g", 0, 0, axis_index_groups=groups, tiled=True)


def half_kernel(other, grad_hbm, attn_hbm, out_ref, grad, attn, grad_sems, attn_sems):
    x, y, core = place(lax.axis_index("g"))
    core = core ^ other
    mine = colour(x, y, core)
    tokens, run = grad.shape[1:]
    cut = tokens // COPIES
    copies = {}
    for x_low in range(2):
        columns = pl.ds(pl.multiple_of((x_low * 2 + core) * run, run), run)
        for part in range(COPIES):
            rows = pl.ds(part * cut, cut)
            if x_low == 0:
                copies["attn", part] = pltpu.make_async_copy(
                    attn_hbm.at[rows, :], attn.at[rows, :], attn_sems.at[part]
                )
                copies["attn", part].start()
            copies[x_low, part] = pltpu.make_async_copy(
                grad_hbm.at[rows, columns], grad.at[x_low, rows, :], grad_sems.at[x_low, part]
            )
            copies[x_low, part].start()
    for x_low, parts in ((0, (0,)), (0, (1,)), (1, (0, 1))):
        for part in parts:
            if x_low == 0:
                copies["attn", part].wait()
            copies[x_low, part].wait()
        rows = slice(parts[0] * cut, (parts[-1] + 1) * cut)
        for k in range(Y):
            block = lax.dot_general(
                grad[x_low, rows, k * 128 : (k + 1) * 128],
                attn[rows, :],
                (((0,), (0,)), ((), ())),
                preferred_element_type=jnp.float32,
            )
            for x_high in range(2):
                x = x_high * 2 + x_low
                at = ((colour(x, k, core) - mine) & 3) * 8 + k
                term = block[x_high * 64 : (x_high + 1) * 64, :]
                out_ref[at] = out_ref[at] + term if parts == (1,) else term


def half(grad_out, attn_out, other):
    tokens, columns = attn_out.shape
    run = grad_out.shape[1] // 4
    return pl.pallas_call(
        functools.partial(half_kernel, other),
        out_shape=jax.ShapeDtypeStruct((X * Y, run // 16, columns), jnp.float32),
        in_specs=[pl.BlockSpec(memory_space=pltpu.HBM)] * 2,
        out_specs=pl.BlockSpec(memory_space=pltpu.VMEM),
        scratch_shapes=[
            pltpu.VMEM((2, tokens, run), jnp.bfloat16),
            pltpu.VMEM((tokens, columns), jnp.bfloat16),
            pltpu.SemaphoreType.DMA((2, COPIES)),
            pltpu.SemaphoreType.DMA((COPIES,)),
        ],
        compiler_params=pltpu.CompilerParams(vmem_limit_bytes=16 << 20),
        cost_estimate=pl.CostEstimate(
            flops=4 * tokens * run * columns,
            bytes_accessed=4 * tokens * run + 2 * tokens * columns + 8 * run * columns,
            transcendentals=0,
        ),
    )(grad_out, attn_out)


def body(grad_out, attn_out):
    factor = 1.0 / math.sqrt(float(grad_out.shape[0] * lax.axis_size("g")))
    grad_out, attn_out = (pltpu.with_memory_space_constraint(v, pltpu.HBM) for v in (grad_out, attn_out))
    theirs = half(grad_out, attn_out, 1)
    got = lax.ppermute(theirs, "g", [(s, s ^ 16) for s in range(2 * X * Y)])
    mine = half(grad_out, attn_out, 0)
    came = []
    for apart in range(1, 4):
        at = slice(apart * 8, apart * 8 + 8)
        came.append(near(mine[at] + got[at], apart))
    total = (mine[:8] + got[:8]) + came[0] + came[1] + came[2]
    terms = far(total)
    total = terms[0]
    for at in range(1, terms.shape[0]):
        total = total + terms[at]
    return total * factor


def solution(mesh):
    cuts, dp, tensor = mesh.devices.shape
    flat = Mesh(mesh.devices.reshape(cuts * dp, tensor), ("g", "z"))
    placed = (P("g", None), P("g", "z"))
    return jax.shard_map(body, mesh=flat, in_specs=placed, out_specs=P("g", "z"), check_vma=False)
```

```python
import functools
import math

import jax
import jax.numpy as jnp
from jax import lax
from jax.experimental import pallas as pl
from jax.experimental.pallas import tpu as pltpu
from jax.sharding import Mesh, PartitionSpec as P


X, Y = 4, 8
COPIES = 2


def place(g):
    return (g & 1) * 2 + (g >> 5), (g >> 1) & 7, (g >> 4) & 1


def position(x, y, core):
    return (((x % 2) * 2 + core) * Y + y) * 2 + x // 2


def colour(x, y, core):
    return (x * (1 - 2 * core) + y * 2) & 3


def near(value, apart):
    dx, dy = {1: (1, 0), 2: (0, 1), 3: (-1, 0)}[apart]
    pairs = []
    for g in range(2 * X * Y):
        x, y, core = place(g)
        to = (x + dx * (1 - 2 * core)) % X, (y + dy * (1 - 2 * core)) % Y
        assert (colour(*to, core) - colour(x, y, core)) % 4 == apart
        pairs.append((g, position(*to, core)))
    return lax.ppermute(value, "g", pairs)


def far(value):
    groups = [[0] * 8 for _ in range(8)]
    for g in range(2 * X * Y):
        x, y, core = place(g)
        groups[core * 4 + colour(x, y, core)][y] = g
    return lax.all_to_all(value, "g", 0, 0, axis_index_groups=groups, tiled=True)


def where(other, apart):
    x, y, core = place(lax.axis_index("g"))
    core = core ^ other
    x_low = (x + apart) & 1
    return x_low * 2 + core, core, x_low, colour(x, y, core)


def multiply(other, apart, rows, grad, first, attn, out_ref, add):
    _, core, x_low, mine = where(other, apart)
    for k in range(Y):
        block = lax.dot_general(
            grad[rows, pl.ds(first + k * 128, 128)],
            attn[rows, :],
            (((0,), (0,)), ((), ())),
            preferred_element_type=jnp.float32,
        )
        for x_high in range(2):
            far_off = (colour(x_high * 2 + x_low, k, core) - mine) & 3
            at = (far_off >> 1) * 8 + k
            term = block[x_high * 64 : (x_high + 1) * 64, :]
            out_ref[at] = out_ref[at] + term if add else term


def first_kernel(other, apart, grad_hbm, attn_hbm, out_ref, grad, attn, sems):
    tokens, run = grad.shape
    columns = pl.ds(pl.multiple_of(where(other, apart)[0] * run, run), run)
    copies = []
    for part in range(COPIES):
        rows = pl.ds(part * (tokens // COPIES), tokens // COPIES)
        for at, (source, target) in enumerate(
            ((attn_hbm.at[rows, :], attn.at[rows, :]), (grad_hbm.at[rows, columns], grad.at[rows, :]))
        ):
            copies.append(pltpu.make_async_copy(source, target, sems.at[part, at]))
            copies[-1].start()
    for part in range(COPIES):
        copies[2 * part].wait()
        copies[2 * part + 1].wait()
        rows = slice(part * (tokens // COPIES), (part + 1) * (tokens // COPIES))
        multiply(other, apart, rows, grad, 0, attn, out_ref, part > 0)


def later_kernel(other, apart, grad_ref, attn_ref, out_ref):
    run = grad_ref.shape[1] // 4
    first = pl.multiple_of(where(other, apart)[0] * run, run)
    multiply(other, apart, slice(None), grad_ref, first, attn_ref, out_ref, False)


def term(grad_out, attn_out, other, apart, first):
    tokens, columns = attn_out.shape
    run = grad_out.shape[1] // 4
    scratch = [
        pltpu.VMEM((tokens, run), jnp.bfloat16),
        pltpu.VMEM((tokens, columns), jnp.bfloat16),
        pltpu.SemaphoreType.DMA((COPIES, 2)),
    ]
    return pl.pallas_call(
        functools.partial(first_kernel if first else later_kernel, other, apart),
        out_shape=jax.ShapeDtypeStruct((X * Y // 2, run // 16, columns), jnp.float32),
        in_specs=[pl.BlockSpec(memory_space=pltpu.HBM if first else pltpu.VMEM)] * 2,
        out_specs=pl.BlockSpec(memory_space=pltpu.VMEM),
        scratch_shapes=scratch if first else [],
        compiler_params=pltpu.CompilerParams(vmem_limit_bytes=8 << 20),
        cost_estimate=pl.CostEstimate(
            flops=2 * tokens * run * columns,
            bytes_accessed=2 * tokens * run + 2 * tokens * columns + 4 * run * columns,
            transcendentals=0,
        ),
    )(grad_out, attn_out)


def body(grad_out, attn_out):
    factor = 1.0 / math.sqrt(float(grad_out.shape[0] * lax.axis_size("g")))
    in_hbm = [pltpu.with_memory_space_constraint(v, pltpu.HBM) for v in (grad_out, attn_out)]
    swap = [(s, s ^ 16) for s in range(2 * X * Y)]
    got_odd = lax.ppermute(term(*in_hbm, 1, 1, True), "g", swap)
    got_even = lax.ppermute(term(grad_out, attn_out, 1, 0, False), "g", swap)
    mine_odd = term(grad_out, attn_out, 0, 1, False)
    one = near(mine_odd[:8] + got_odd[:8], 1)
    three = near(mine_odd[8:] + got_odd[8:], 3)
    mine_even = term(grad_out, attn_out, 0, 0, False)
    two = near(mine_even[8:] + got_even[8:], 2)
    total = (mine_even[:8] + got_even[:8]) + one + three + two
    terms = far(total)
    total = terms[0]
    for at in range(1, terms.shape[0]):
        total = total + terms[at]
    return total * factor


def solution(mesh):
    cuts, dp, tensor = mesh.devices.shape
    flat = Mesh(mesh.devices.reshape(cuts * dp, tensor), ("g", "z"))
    placed = (P("g", None), P("g", "z"))
    return jax.shard_map(body, mesh=flat, in_specs=placed, out_specs=P("g", "z"), check_vma=False)
```
